1024 devices in a mesh: pb: 128 (over y, z), row: 8 (over x, core).
Axes of the slice: x: 4, y: 4, z: 32, core: 2. Of those that a mesh axis runs over, the one named last changes fastest.
Arguments:
- orbitals: bfloat16 [128, 1280, 128], P('pb', 'row'), may hold values from -4 to 4
- interaction: bfloat16 [2, 128, 1280, 1280], P(None, 'pb', 'row'), may hold values from -0.078125 to 0.078125
- pair_list: int32 [128, 3, 2], P('pb'), may hold values from 0 to 127, as said below
- flag_list: int32 [128, 3], P('pb'), may hold values from 0 to 1
- pair_counts: int32 [128], P('pb'), may hold values from 1 to 3, as said below
Outputs:
- exchange_terms: float32 [128, 3, 1280, 128], P('pb', None, 'row')
The draws below stay inside these ranges and needn't reach their ends.
Inputs may be any that keep to these rules, and one draw needn't show every extreme that they name: pair_list[q, s, 1] = (pair_list[q, s, 0] - q) mod 128. `pair_counts`: some q has all 3 slots live.
All inputs are finite; a program needn't handle non-finite values.
Results may differ from the reference program's by a relative error of at most 0.0029.
Values may be sent and summed in bfloat16 or wider, within the bound.
A program may use at most 32 MiB of HBM per device.

```python
import jax
import jax.numpy as jnp
from jax import lax

NMU = 1280
NB = 64
PAIRS = 3
NQ = 128
NK = 128


def draw_pair_list(key, part):
    first_ids = jax.random.randint(key, (NQ, PAIRS), 0, NK)
    group_index = jnp.arange(NQ, dtype=jnp.int32)[:, None]
    second_ids = (first_ids - group_index) % NK
    return jnp.stack([first_ids, second_ids], axis=2).astype(jnp.int32)


def draw_pair_counts(key, part):
    values = jax.random.randint(key, (NQ,), 1, PAIRS + 1)
    return values.at[0].set(PAIRS).astype(jnp.int32)


def plant(result, own_key, least, high):
    shape = result.shape
    index_at = [jax.random.randint(jax.random.fold_in(own_key, axis), (), 0, shape[axis]) for axis in range(len(shape))]
    result = result.at[tuple(index_at)].set(least)
    longest = shape.index(max(shape))
    index_at[longest] = (index_at[longest] + 1) % shape[longest]
    return result.at[tuple(index_at)].set(high)


def block_scale(stream_key, extent, pieces, low, high):
    gain = 1.0
    for position, blocks in pieces:
        heights = jax.random.uniform(jax.random.fold_in(jax.random.fold_in(stream_key, 6), position), (blocks,), jnp.float32, low / len(pieces), high / len(pieces))
        gain = gain * jnp.repeat(jnp.exp(heights), extent[position] // blocks).reshape((-1,) + (1,) * (len(extent) - 1 - position))
    return gain


def scatter_about(stream_key, dims, scale, reach, pieces=(), kind=jnp.bfloat16):
    entries = jax.random.normal(stream_key, dims, jnp.float32) * scale
    if len(pieces) > 0:
        entries = block_scale(stream_key, dims, pieces, -0.22, 0.18) * entries
    return jnp.clip(entries, min=-reach, max=reach).astype(kind)


def setup_inputs(seed: int = 0) -> dict:
    splits = jax.random.split(jax.random.key(seed), 6)
    orbitals = scatter_about(splits[0], (NK, NMU, 2 * NB), 0.5, 4.0, ((0, 128), (1, 8)))
    interaction = scatter_about(splits[1], (2, NQ, NMU, NMU), (4 * NMU) ** -0.5, 0.078125, ((1, 128), (2, 8)))
    pair_list = draw_pair_list(jax.random.fold_in(splits[5], 71), 0)
    flag_list = plant(jax.random.randint(splits[3], (NQ, PAIRS), 0, 2), jax.random.fold_in(splits[3], 1), 0, 1).astype(jnp.int32)
    pair_counts = draw_pair_counts(jax.random.fold_in(splits[5], 71), 0)
    return {"orbitals": orbitals, "interaction": interaction, "pair_list": pair_list, "flag_list": flag_list, "pair_counts": pair_counts}


def rotate_parts(block):
    half_width = block.shape[1] // 2
    return jnp.concatenate([block[:, half_width:], -block[:, :half_width]], axis=1)


def apply_kernel(kern_real, kern_imag, target):
    half_width = target.shape[1] // 2
    prod_real = jnp.dot(kern_real, target, preferred_element_type=jnp.float32)
    prod_imag = jnp.dot(kern_imag, target, preferred_element_type=jnp.float32)
    return jnp.concatenate([prod_real[:, :half_width] - prod_imag[:, half_width:],
                            prod_real[:, half_width:] + prod_imag[:, :half_width]], axis=1)


def reference(orbitals, interaction, pair_list, flag_list, pair_counts):
    def one_group(inputs):
        w_real, w_imag, group_pairs, group_flags, group_count = inputs
        results = []
        for slot_index in range(PAIRS):
            target = orbitals[group_pairs[slot_index, 0]]
            source = orbitals[group_pairs[slot_index, 1]]
            dens_real = jnp.dot(source, source.T, preferred_element_type=jnp.float32)
            dens_imag = jnp.dot(rotate_parts(source), source.T, preferred_element_type=jnp.float32)
            adjoint = group_flags[slot_index] == 1
            eff_real = jnp.where(adjoint, w_real.T, w_real)
            eff_imag = jnp.where(adjoint, -w_imag.T, w_imag)
            kern_real = (eff_real * dens_real - eff_imag * dens_imag).astype(jnp.bfloat16)
            kern_imag = (eff_real * dens_imag + eff_imag * dens_real).astype(jnp.bfloat16)
            active = (slot_index < group_count).astype(jnp.float32)
            results.append(apply_kernel(kern_real, kern_imag, target) * active)
        return jnp.stack(results)
    return lax.map(one_group, (interaction[0], interaction[1], pair_list, flag_list, pair_counts))
```

```python
import functools

import jax
import jax.numpy as jnp
from jax import lax
from jax.experimental import pallas as pl
from jax.experimental.pallas import tpu as pltpu
from jax.sharding import PartitionSpec as P

MESH = pl.DeviceIdType.MESH
NY = 4
CORES = 2
CHUNKS = 2


def gather_kernel(
    ny, nz, nx,
    pair_ref, orb_ref, w_ref,
    full_ref, wcol_ref,
    ring, chosen, wsend, idx_send, idx_all, idx_smem,
    idx_ss, idx_rs, piece_ss, piece_rs, z_ss, z_rs, y_ss, y_rs,
    x_ss, x_rs, hop_ss, hop_rs, core_ss, core_rs, w_ss, w_rs, local_sem,
):
    slots = pair_ref.shape[1]
    wanted = 2 * slots
    pb = lax.axis_index("pb")
    row = lax.axis_index("row")
    y, z = lax.div(pb, nz), lax.rem(pb, nz)
    x, core = lax.div(row, CORES), lax.rem(row, CORES)
    rows = nx * CORES

    def y_peer(d):
        return lax.rem(y + d, ny)

    def z_peer(d):
        return lax.rem(z + d + nz, nz)

    def row_peer(d):
        return lax.rem(row + d, rows)

    def remote(src, dst, ss, rs, to_pb, to_row):
        return pltpu.make_async_remote_copy(
            src_ref=src, dst_ref=dst, send_sem=ss, recv_sem=rs,
            device_id=(to_pb, to_row), device_id_type=MESH,
        )

    barrier = pltpu.get_barrier_semaphore()
    partners = [(y_peer(d) * nz + z, row) for d in range(1, ny)]
    z_steps = (1, -1) if nz > 2 else (1,)
    partners += [(y * nz + z_peer(d), row) for d in z_steps]
    partners += [(pb, row_peer(d)) for d in range(1, rows)]
    for partner in partners:
        pl.semaphore_signal(barrier, inc=1, device_id=partner, device_id_type=MESH)
    pl.semaphore_wait(barrier, len(partners))

    def piece_copy(d):
        to = y_peer(d)
        return remote(
            orb_ref.at[to], ring.at[z, y], piece_ss.at[d - 1], piece_rs.at[d - 1], to * nz + z, row
        )

    for d in range(1, ny):
        piece_copy(d).start()

    lane = lax.broadcasted_iota(jnp.int32, idx_send.shape, 1)
    table = jnp.zeros(idx_send.shape, jnp.int32)
    for j in range(wanted):
        table = jnp.where(lane == j, pair_ref[0, j % slots, j // slots], table)
    idx_send[...] = table
    idx_all[y] = table
    ring[z, y] = orb_ref[y]

    def idx_copy(d):
        to = y_peer(d)
        return remote(
            idx_send, idx_all.at[y], idx_ss.at[d - 1], idx_rs.at[d - 1], to * nz + z, row
        )

    for d in range(1, ny):
        idx_copy(d).start()

    for d in range(1, ny):
        piece_copy(d).wait_recv()

    half = nz // 2
    width = ny // CHUNKS

    def z_copy(way, step, part):
        block = lax.rem(z - step + nz, nz) if way == 0 else lax.rem(z + step, nz)
        view = ring.at[block, pl.ds(part * width, width)]
        return remote(
            view, view, z_ss.at[way, step, part], z_rs.at[way, step, part],
            y * nz + z_peer(1 if way == 0 else -1), row,
        )

    def last(way, part):
        return (part < CHUNKS // 2) == (way == 0)

    pairs = [(way, part) for part in range(CHUNKS) for way in range(2)]
    for way, part in pairs:
        if half > 1 or last(way, part):
            z_copy(way, 0, part).start()

    span = wsend.shape[-1]
    for p in range(rows):
        wsend[p] = w_ref[:, :, p * span : (p + 1) * span]

    def w_copy(d):
        to = row_peer(d)
        return remote(wsend.at[to], wcol_ref.at[row], w_ss.at[d - 1], w_rs.at[d - 1], pb, to)

    for d in range(1, rows):
        w_copy(d).start()
    own_columns = pltpu.make_async_copy(wsend.at[row], wcol_ref.at[row], local_sem.at[0])
    own_columns.start()

    def z_step(step, carry):
        for way, part in pairs:
            z_copy(way, step - 1, part).wait_recv()
            z_copy(way, step, part).start()
        return carry

    if half > 1:
        lax.fori_loop(1, half - 1, z_step, 0)
        for way, part in pairs:
            z_copy(way, half - 2, part).wait_recv()
            if last(way, part):
                z_copy(way, half - 1, part).start()

    for d in range(1, ny):
        idx_copy(d).wait_recv()
    to_smem = pltpu.make_async_copy(idx_all, idx_smem, local_sem.at[1])
    to_smem.start()
    to_smem.wait()

    for way, part in pairs:
        if last(way, part):
            z_copy(way, half - 1, part).wait_recv()

    def y_copy(d):
        to = y_peer(d)
        return remote(
            chosen.at[d - 1], full_ref.at[:, row, y], y_ss.at[d - 1], y_rs.at[d - 1], to * nz + z, row
        )

    for d in range(1, ny):
        to = y_peer(d)
        for j in range(wanted):
            k = idx_smem[to, 0, j]
            chosen[d - 1, j] = ring[lax.rem(k, nz), lax.div(k, nz)]
        y_copy(d).start()
    for j in range(wanted):
        k = idx_smem[y, 0, j]
        full_ref[j, row, y] = ring[lax.rem(k, nz), lax.div(k, nz)]
    for d in range(1, ny):
        y_copy(d).wait_recv()

    other = 1 - core

    def part_of(part, at):
        return full_ref.at[pl.ds(part * slots, slots), at]

    def at_x(d):
        return lax.rem(x + d + nx, nx) * CORES + core

    def x_copy(way, part):
        view = part_of(part, row)
        return remote(
            view, view, x_ss.at[way, part], x_rs.at[way, part], pb, at_x(1 if way == 0 else -1)
        )

    def hop_copy(way):
        view = part_of(1 - way, at_x(-1 if way == 0 else 1))
        return remote(
            view, view, hop_ss.at[way], hop_rs.at[way], pb, at_x(1 if way == 0 else -1)
        )

    def core_copy(d, part):
        view = part_of(part, at_x(d))
        return remote(
            view, view, core_ss.at[d, part], core_rs.at[d, part], pb, x * CORES + other
        )

    if nx == 4:
        for part in (1, 0):
            for way in range(2):
                x_copy(way, part).start()
        for part in (1, 0):
            core_copy(0, part).start()
        for part in (1, 0):
            for way in range(2):
                x_copy(way, part).wait_recv()
                if part == 1 - way:
                    hop_copy(way).start()
                core_copy(3 if way == 0 else 1, part).start()
        for way in range(2):
            hop_copy(way).wait_recv()
            core_copy(2, 1 - way).start()
    else:
        for part in (1, 0):
            core_copy(0, part).start()
    for d in range(nx):
        for part in (1, 0):
            core_copy(d, part).wait_recv()

    own_columns.wait()
    for d in range(1, rows):
        w_copy(d).wait()
    for d in range(1, ny):
        piece_copy(d).wait_send()
        idx_copy(d).wait_send()
        y_copy(d).wait_send()

    def z_drain(step, carry):
        for way, part in pairs:
            z_copy(way, step, part).wait_send()
        return carry

    lax.fori_loop(0, half - 1, z_drain, 0)
    for way, part in pairs:
        if last(way, part):
            z_copy(way, half - 1, part).wait_send()
    if nx == 4:
        for part in (1, 0):
            for way in range(2):
                x_copy(way, part).wait_send()
        for way in range(2):
            hop_copy(way).wait_send()
    for d in range(nx):
        for part in (1, 0):
            core_copy(d, part).wait_send()


def gather(ny, pb_total, rows, pair_list, orbitals, w):
    nz, nx = pb_total // ny, rows // CORES
    slots = pair_list.shape[1]
    piece, width = orbitals.shape[1:]
    span = w.shape[2] // rows
    dma = pltpu.SemaphoreType.DMA
    half = nz // 2
    vmem = pl.BlockSpec(memory_space=pltpu.VMEM)
    sent = 12 * orbitals.size * 2
    return pl.pallas_call(
        functools.partial(gather_kernel, ny, nz, nx),
        out_shape=(
            jax.ShapeDtypeStruct((2 * slots, rows, ny, piece, width), jnp.bfloat16),
            jax.ShapeDtypeStruct((rows, 2, w.shape[1], span), jnp.bfloat16),
        ),
        in_specs=[pl.BlockSpec(memory_space=pltpu.SMEM), vmem, vmem],
        out_specs=(vmem, vmem),
        scratch_shapes=[
            pltpu.VMEM((nz, ny, piece, width), jnp.bfloat16),
            pltpu.VMEM((ny - 1, 2 * slots, piece, width), jnp.bfloat16),
            pltpu.VMEM((rows, 2, w.shape[1], span), jnp.bfloat16),
            pltpu.VMEM((8, 128), jnp.int32),
            pltpu.VMEM((ny, 8, 128), jnp.int32),
            pltpu.SMEM((ny, 8, 128), jnp.int32),
            dma((ny - 1,)), dma((ny - 1,)),
            dma((ny - 1,)), dma((ny - 1,)),
            dma((2, half, CHUNKS)), dma((2, half, CHUNKS)),
            dma((ny - 1,)), dma((ny - 1,)),
            dma((2, 2)), dma((2, 2)),
            dma((2,)), dma((2,)),
            dma((nx, 2)), dma((nx, 2)),
            dma((rows - 1,)), dma((rows - 1,)),
            dma((2,)),
        ],
        compiler_params=pltpu.CompilerParams(collective_id=0, has_side_effects=True),
        name="gather_orbitals",
    )(pair_list, orbitals, w)


def dot_t(a, b):
    return lax.dot_general(a, b, (((1,), (1,)), ((), ())), preferred_element_type=jnp.float32)


def rotate(block):
    half = block.shape[1] // 2
    return jnp.concatenate([block[:, half:], -block[:, :half]], axis=1)


def exchange_kernel(flag_ref, count_ref, place_ref, full_ref, w_ref, wcol_ref, out_ref):
    slots, local, width = out_ref.shape
    rows = full_ref.shape[1]
    half = width // 2
    total = w_ref.shape[2]
    tile = 256
    me = place_ref[0]

    for s in range(slots):
        live = s < count_ref[0]
        adjoint = flag_ref[0, s] == 1

        @pl.when(jnp.logical_and(live, jnp.logical_not(adjoint)))
        def _(s=s):
            mine = full_ref[slots + s, pl.ds(pl.multiple_of(me * local, local), local), :]
            turned = rotate(mine)
            prod_re = jnp.zeros((local, width), jnp.float32)
            prod_im = jnp.zeros((local, width), jnp.float32)
            for c in range(total // tile):
                cols = pl.ds(c * tile, tile)
                source = full_ref[slots + s, cols, :]
                target = full_ref[s, cols, :]
                d_re = dot_t(mine, source)
                d_im = dot_t(turned, source)
                w_re = w_ref[0, :, cols].astype(jnp.float32)
                w_im = w_ref[1, :, cols].astype(jnp.float32)
                k_re = (w_re * d_re - w_im * d_im).astype(jnp.bfloat16)
                k_im = (w_re * d_im + w_im * d_re).astype(jnp.bfloat16)
                prod_re += jnp.dot(k_re, target, preferred_element_type=jnp.float32)
                prod_im += jnp.dot(k_im, target, preferred_element_type=jnp.float32)
            out_ref[s, :, :half] = prod_re[:, :half] - prod_im[:, half:]
            out_ref[s, :, half:] = prod_re[:, half:] + prod_im[:, :half]

        @pl.when(jnp.logical_and(live, adjoint))
        def _(s=s):
            mine = full_ref[slots + s, pl.ds(pl.multiple_of(me * local, local), local), :]
            prod_re = jnp.zeros((width, local), jnp.float32)
            prod_im = jnp.zeros((width, local), jnp.float32)
            for p in range(wcol_ref.shape[0]):
                cols = pl.ds(p * local, local)
                source = full_ref[slots + s, cols, :]
                target = full_ref[s, cols, :]
                d_re = dot_t(source, mine)
                d_im = dot_t(rotate(source), mine)
                w_re = wcol_ref[p, 0].astype(jnp.float32)
                w_im = wcol_ref[p, 1].astype(jnp.float32)
                k_re = (w_re * d_re - w_im * d_im).astype(jnp.bfloat16)
                k_im = (w_re * d_im + w_im * d_re).astype(jnp.bfloat16)
                flip = target.T
                prod_re += jnp.dot(flip, k_re, preferred_element_type=jnp.float32)
                prod_im += jnp.dot(flip, k_im, preferred_element_type=jnp.float32)
            top = prod_re[:half] + prod_im[half:]
            bottom = prod_re[half:] - prod_im[:half]
            out_ref[s] = jnp.concatenate([top, bottom], axis=0).T

        @pl.when(jnp.logical_not(live))
        def _(s=s):
            out_ref[s] = jnp.zeros((local, width), jnp.float32)


def exchange(flag_list, pair_counts, place, full, w, wcol):
    slots = full.shape[0] // 2
    local, width = w.shape[1], full.shape[2]
    smem = pl.BlockSpec(memory_space=pltpu.SMEM)
    vmem = pl.BlockSpec(memory_space=pltpu.VMEM)
    return pl.pallas_call(
        exchange_kernel,
        out_shape=jax.ShapeDtypeStruct((slots, local, width), jnp.float32),
        in_specs=[smem, smem, smem, vmem, vmem, vmem],
        out_specs=vmem,
        name="exchange_terms",
    )(flag_list, pair_counts, place, full, w, wcol)


def shards(ny, pb_total, rows, orbitals, interaction, pair_list, flag_list, pair_counts):
    local, width = orbitals.shape[1:]
    w = interaction[:, 0]
    pieces = orbitals.reshape(ny, local // ny, width)
    full, wcol = gather(ny, pb_total, rows, pair_list, pieces, w)
    full = full.reshape(full.shape[0], rows * local, width)
    place = lax.axis_index("row").astype(jnp.int32).reshape(1)
    return exchange(flag_list, pair_counts, place, full, w, wcol)[None]


def solution(mesh, ny=NY):
    return jax.shard_map(
        functools.partial(shards, ny, mesh.shape["pb"], mesh.shape["row"]),
        mesh=mesh,
        in_specs=(
            P("pb", "row", None),
            P(None, "pb", "row", None),
            P("pb", None, None),
            P("pb", None),
            P("pb"),
        ),
        out_specs=P("pb", None, "row", None),
        check_vma=False,
    )
```

```python
import functools

import jax
import jax.numpy as jnp
from jax import lax
from jax.experimental import pallas as pl
from jax.experimental.pallas import tpu as pltpu
from jax.sharding import PartitionSpec as P

MESH = pl.DeviceIdType.MESH
NY = 4
CORES = 2
LANES = 128
CHUNKS = 2
GROUP = 2


def gather_kernel(
    ny, nz, nx, group,
    pair_ref, orb_ref, w_ref,
    full_ref, wcol_ref,
    ring, chosen, wsend, idx_send, idx_all, idx_smem,
    idx_ss, idx_rs, piece_ss, piece_rs, z_ss, z_rs, sib_ss, sib_rs, own_ss, own_rs, y_ss, y_rs,
    x_ss, x_rs, hop_ss, hop_rs, core_ss, core_rs, w_ss, w_rs, local_sem,
):
    slots = pair_ref.shape[2]
    wanted = 2 * slots
    pb = lax.axis_index("pb")
    row = lax.axis_index("row")
    y, z = lax.div(pb, nz), lax.rem(pb, nz)
    x, core = lax.div(row, CORES), lax.rem(row, CORES)
    rows = nx * CORES
    stops = nz // group
    stop, seat = lax.div(z, group), lax.rem(z, group)
    kind = lax.rem(row, group)
    base = row - kind
    t_z, t_row = stop * group + kind, base + seat
    same = seat == kind
    moved = jnp.logical_not(same)

    def y_peer(d):
        return lax.rem(y + d, ny)

    def z_peer(d):
        return lax.rem(z + d * group + nz, nz)

    def row_peer(d):
        return lax.rem(row + d, rows)

    def remote(src, dst, ss, rs, to_pb, to_row):
        return pltpu.make_async_remote_copy(
            src_ref=src, dst_ref=dst, send_sem=ss, recv_sem=rs,
            device_id=(to_pb, to_row), device_id_type=MESH,
        )

    barrier = pltpu.get_barrier_semaphore()
    partners = [(y_peer(d) * nz + t_z, t_row) for d in range(1, ny)]
    ways = (1, -1) if stops > 2 else (1,)
    partners += [(y * nz + z_peer(d), row) for d in ways]
    partners += [(pb, row_peer(d)) for d in range(1, rows)]
    for partner in partners:
        pl.semaphore_signal(barrier, inc=1, device_id=partner, device_id_type=MESH)

    @pl.when(moved)
    def _():
        pl.semaphore_signal(
            barrier, inc=1, device_id=(y * nz + t_z, t_row), device_id_type=MESH
        )
        pl.semaphore_wait(barrier, len(partners) + 1)

    @pl.when(same)
    def _():
        pl.semaphore_wait(barrier, len(partners))

    def to_swap(src, dst, ss, rs, d):
        return remote(src, dst, ss.at[d], rs.at[d], y_peer(d) * nz + t_z, t_row)

    def piece_copy(d):
        return to_swap(orb_ref.at[y_peer(d)], ring.at[seat, stop, y], piece_ss, piece_rs, d)

    def idx_copy(d):
        return to_swap(idx_send, idx_all.at[y], idx_ss, idx_rs, d)

    @pl.when(moved)
    def _():
        piece_copy(0).start()

    for d in range(1, ny):
        piece_copy(d).start()

    lane = lax.broadcasted_iota(jnp.int32, idx_send.shape, 1)
    table = jnp.zeros(idx_send.shape, jnp.int32)
    for j in range(wanted):
        table = jnp.where(lane == j, pair_ref[0, j // slots, j % slots], table)
    idx_send[...] = table

    @pl.when(same)
    def _():
        idx_all[y] = table
        ring[seat, stop, y] = orb_ref[y]

    @pl.when(moved)
    def _():
        idx_copy(0).start()

    for d in range(1, ny):
        idx_copy(d).start()

    @pl.when(moved)
    def _():
        piece_copy(0).wait_recv()

    for d in range(1, ny):
        piece_copy(d).wait_recv()

    half = stops // 2
    width = ny // CHUNKS

    def block_at(way, step):
        return lax.rem(stop - step + stops, stops) if way == 0 else lax.rem(stop + step, stops)

    def z_copy(way, step, part):
        view = ring.at[kind, block_at(way, step), pl.ds(part * width, width)]
        return remote(
            view, view, z_ss.at[way, step, part], z_rs.at[way, step, part],
            y * nz + z_peer(1 if way == 0 else -1), row,
        )

    def sibling(d):
        return base + lax.rem(kind + d, group)

    def sib_copy(d, way, step, part):
        view = ring.at[kind, block_at(way, step + 1), pl.ds(part * width, width)]
        return remote(
            view, view, sib_ss.at[d - 1, way, step, part], sib_rs.at[d - 1, way, step, part],
            pb, sibling(d),
        )

    def own_copy(d):
        view = ring.at[kind, stop]
        return remote(view, view, own_ss.at[d - 1], own_rs.at[d - 1], pb, sibling(d))

    others = range(1, group)

    def last(way, part):
        return (part < CHUNKS // 2) == (way == 0)

    pairs = [(way, part) for part in range(CHUNKS) for way in range(2)]
    for way, part in pairs:
        if half > 1 or last(way, part):
            z_copy(way, 0, part).start()
    for d in others:
        own_copy(d).start()

    span, local = w_ref.shape[2] // rows, w_ref.shape[1]
    folds = LANES // (span - LANES)
    fold = local // folds
    for p in range(rows):
        split = p * span + LANES
        wsend[p, :, :local] = w_ref[:, :, p * span : split]
        rest = w_ref[:, :, split : (p + 1) * span].astype(jnp.float32)
        wsend[p, :, local:] = jnp.concatenate(
            [rest[:, f * fold : (f + 1) * fold] for f in range(folds)], axis=2
        ).astype(jnp.bfloat16)

    def w_copy(d):
        to = row_peer(d)
        return remote(wsend.at[to], wcol_ref.at[row], w_ss.at[d - 1], w_rs.at[d - 1], pb, to)

    for d in range(1, rows):
        w_copy(d).start()
    own_columns = pltpu.make_async_copy(wsend.at[row], wcol_ref.at[row], local_sem.at[0])
    own_columns.start()

    def z_step(step, carry):
        for way, part in pairs:
            z_copy(way, step - 1, part).wait_recv()
            z_copy(way, step, part).start()
            for d in others:
                sib_copy(d, way, step - 1, part).start()
        return carry

    if half > 1:
        lax.fori_loop(1, half - 1, z_step, 0)
        for way, part in pairs:
            z_copy(way, half - 2, part).wait_recv()
            if last(way, part):
                z_copy(way, half - 1, part).start()
            for d in others:
                sib_copy(d, way, half - 2, part).start()

    @pl.when(moved)
    def _():
        idx_copy(0).wait_recv()

    for d in range(1, ny):
        idx_copy(d).wait_recv()
    to_smem = pltpu.make_async_copy(idx_all, idx_smem, local_sem.at[1])
    to_smem.start()
    to_smem.wait()

    for way, part in pairs:
        if last(way, part):
            z_copy(way, half - 1, part).wait_recv()
            for d in others:
                sib_copy(d, way, half - 1, part).start()

    def sib_wait(step, carry):
        for way, part in pairs:
            for d in others:
                sib_copy(d, way, step, part).wait_recv()
        return carry

    if group > 1:
        for d in others:
            own_copy(d).wait_recv()
        lax.fori_loop(0, half - 1, sib_wait, 0)
        for way, part in pairs:
            if last(way, part):
                for d in others:
                    sib_copy(d, way, half - 1, part).wait_recv()

    def y_copy(d, j):
        return remote(
            chosen.at[d, j], full_ref.at[j, t_row, y], y_ss.at[d, j], y_rs.at[d, j],
            y_peer(d) * nz + t_z, t_row,
        )

    def listed(at, j):
        k = idx_smem[at, 0, j]
        k_z = lax.rem(k, nz)
        return ring[lax.rem(k_z, group), lax.div(k_z, group), lax.div(k, nz)]

    for j in range(wanted):
        for d in range(ny):
            chosen[d, j] = listed(y_peer(d), j)
        for d in range(1, ny):
            y_copy(d, j).start()

        @pl.when(moved)
        def _(j=j):
            y_copy(0, j).start()

        @pl.when(same)
        def _(j=j):
            full_ref[j, row, y] = chosen[0, j]

    other = 1 - core

    def at_x(d):
        return lax.rem(x + d + nx, nx) * CORES + core

    def x_copy(way, j):
        view = full_ref.at[j, row]
        return remote(
            view, view, x_ss.at[way, j], x_rs.at[way, j], pb, at_x(1 if way == 0 else -1)
        )

    def hop_copy(j):
        ahead = 1 if j % 2 == 0 else -1
        view = full_ref.at[j, at_x(-ahead)]
        return remote(view, view, hop_ss.at[j], hop_rs.at[j], pb, at_x(ahead))

    def core_copy(d, j):
        view = full_ref.at[j, at_x(d)]
        return remote(
            view, view, core_ss.at[d, j], core_rs.at[d, j], pb, x * CORES + other
        )

    for j in range(wanted):
        for d in range(1, ny):
            y_copy(d, j).wait_recv()

        @pl.when(moved)
        def _(j=j):
            y_copy(0, j).wait_recv()

        if nx == 4:
            for way in range(2):
                x_copy(way, j).start()
        core_copy(0, j).start()
    if nx == 4:
        for j in range(wanted):
            for way in (0, 1) if j % 2 == 0 else (1, 0):
                x_copy(way, j).wait_recv()
                if way == j % 2:
                    hop_copy(j).start()
                core_copy(3 if way == 0 else 1, j).start()
        for j in range(wanted):
            hop_copy(j).wait_recv()
            core_copy(2, j).start()
    for j in range(wanted):
        for d in range(nx):
            core_copy(d, j).wait_recv()

    own_columns.wait()
    for d in range(1, rows):
        w_copy(d).wait()
    @pl.when(moved)
    def _():
        piece_copy(0).wait_send()
        idx_copy(0).wait_send()
        for j in range(wanted):
            y_copy(0, j).wait_send()

    for d in others:
        own_copy(d).wait_send()
    for d in range(1, ny):
        piece_copy(d).wait_send()
        idx_copy(d).wait_send()
        for j in range(wanted):
            y_copy(d, j).wait_send()

    def z_drain(step, carry):
        for way, part in pairs:
            z_copy(way, step, part).wait_send()
            for d in others:
                sib_copy(d, way, step, part).wait_send()
        return carry

    lax.fori_loop(0, half - 1, z_drain, 0)
    for way, part in pairs:
        if last(way, part):
            z_copy(way, half - 1, part).wait_send()
            for d in others:
                sib_copy(d, way, half - 1, part).wait_send()
    for j in range(wanted):
        if nx == 4:
            for way in range(2):
                x_copy(way, j).wait_send()
            hop_copy(j).wait_send()
        for d in range(nx):
            core_copy(d, j).wait_send()


def gather(ny, pb_total, rows, pair_list, orbitals, w):
    nz, nx = pb_total // ny, rows // CORES
    slots = pair_list.shape[2]
    stops = nz // GROUP
    siblings = max(GROUP - 1, 1)
    piece, width = orbitals.shape[1:]
    span = w.shape[2] // rows
    packed = w.shape[1] * span // LANES
    dma = pltpu.SemaphoreType.DMA
    half = stops // 2
    vmem = pl.BlockSpec(memory_space=pltpu.VMEM)
    return pl.pallas_call(
        functools.partial(gather_kernel, ny, nz, nx, GROUP),
        out_shape=(
            jax.ShapeDtypeStruct((2 * slots, rows, ny, piece, width), jnp.bfloat16),
            jax.ShapeDtypeStruct((rows, 2, packed, LANES), jnp.bfloat16),
        ),
        in_specs=[pl.BlockSpec(memory_space=pltpu.SMEM), vmem, vmem],
        out_specs=(vmem, vmem),
        scratch_shapes=[
            pltpu.VMEM((GROUP, stops, ny, piece, width), jnp.bfloat16),
            pltpu.VMEM((ny, 2 * slots, piece, width), jnp.bfloat16),
            pltpu.VMEM((rows, 2, packed, LANES), jnp.bfloat16),
            pltpu.VMEM((8, 128), jnp.int32),
            pltpu.VMEM((ny, 8, 128), jnp.int32),
            pltpu.SMEM((ny, 8, 128), jnp.int32),
            dma((ny,)), dma((ny,)),
            dma((ny,)), dma((ny,)),
            dma((2, half, CHUNKS)), dma((2, half, CHUNKS)),
            dma((siblings, 2, half, CHUNKS)), dma((siblings, 2, half, CHUNKS)),
            dma((siblings,)), dma((siblings,)),
            dma((ny, 2 * slots)), dma((ny, 2 * slots)),
            dma((2, 2 * slots)), dma((2, 2 * slots)),
            dma((2 * slots,)), dma((2 * slots,)),
            dma((nx, 2 * slots)), dma((nx, 2 * slots)),
            dma((rows - 1,)), dma((rows - 1,)),
            dma((2,)),
        ],
        compiler_params=pltpu.CompilerParams(collective_id=0, has_side_effects=True, vmem_limit_bytes=16 << 20),
        name="gather_orbitals",
    )(pair_list, orbitals, w)


def dot_t(a, b):
    return lax.dot_general(a, b, (((1,), (1,)), ((), ())), preferred_element_type=jnp.float32)


def rotate(block):
    half = block.shape[1] // 2
    return jnp.concatenate([block[:, half:], -block[:, :half]], axis=1)


def columns_of(wcol_ref, p, part, local):
    first = wcol_ref[p, part, :local].astype(jnp.float32)
    rest = wcol_ref[p, part, local:].astype(jnp.float32)
    wide = local - LANES
    rest = jnp.concatenate(
        [rest[:, f * wide : (f + 1) * wide] for f in range(LANES // wide)], axis=0
    )
    return jnp.concatenate([first, rest], axis=1)


def exchange_kernel(flag_ref, count_ref, place_ref, full_ref, w_ref, wcol_ref, out_ref):
    slots, local, width = out_ref.shape
    rows = full_ref.shape[1]
    half = width // 2
    total = w_ref.shape[2]
    tile = 256
    me = place_ref[0]

    for s in range(slots):
        live = s < count_ref[0]
        adjoint = flag_ref[0, s] == 1

        @pl.when(jnp.logical_and(live, jnp.logical_not(adjoint)))
        def _(s=s):
            mine = full_ref[slots + s, pl.ds(pl.multiple_of(me * local, local), local), :]
            turned = rotate(mine)
            prod_re = jnp.zeros((local, width), jnp.float32)
            prod_im = jnp.zeros((local, width), jnp.float32)
            for c in range(total // tile):
                cols = pl.ds(c * tile, tile)
                source = full_ref[slots + s, cols, :]
                target = full_ref[s, cols, :]
                d_re = dot_t(mine, source)
                d_im = dot_t(turned, source)
                w_re = w_ref[0, :, cols].astype(jnp.float32)
                w_im = w_ref[1, :, cols].astype(jnp.float32)
                k_re = (w_re * d_re - w_im * d_im).astype(jnp.bfloat16)
                k_im = (w_re * d_im + w_im * d_re).astype(jnp.bfloat16)
                prod_re += jnp.dot(k_re, target, preferred_element_type=jnp.float32)
                prod_im += jnp.dot(k_im, target, preferred_element_type=jnp.float32)
            out_ref[s, :, :half] = prod_re[:, :half] - prod_im[:, half:]
            out_ref[s, :, half:] = prod_re[:, half:] + prod_im[:, :half]

        @pl.when(jnp.logical_and(live, adjoint))
        def _(s=s):
            mine = full_ref[slots + s, pl.ds(pl.multiple_of(me * local, local), local), :]
            prod_re = jnp.zeros((width, local), jnp.float32)
            prod_im = jnp.zeros((width, local), jnp.float32)
            for p in range(wcol_ref.shape[0]):
                cols = pl.ds(p * local, local)
                source = full_ref[slots + s, cols, :]
                target = full_ref[s, cols, :]
                d_re = dot_t(source, mine)
                d_im = dot_t(rotate(source), mine)
                w_re = columns_of(wcol_ref, p, 0, local)
                w_im = columns_of(wcol_ref, p, 1, local)
                k_re = (w_re * d_re - w_im * d_im).astype(jnp.bfloat16)
                k_im = (w_re * d_im + w_im * d_re).astype(jnp.bfloat16)
                flip = target.T
                prod_re += jnp.dot(flip, k_re, preferred_element_type=jnp.float32)
                prod_im += jnp.dot(flip, k_im, preferred_element_type=jnp.float32)
            top = prod_re[:half] + prod_im[half:]
            bottom = prod_re[half:] - prod_im[:half]
            out_ref[s] = jnp.concatenate([top, bottom], axis=0).T

        @pl.when(jnp.logical_not(live))
        def _(s=s):
            out_ref[s] = jnp.zeros((local, width), jnp.float32)


def exchange(flag_list, pair_counts, place, full, w, wcol):
    slots = full.shape[0] // 2
    local, width = w.shape[1], full.shape[2]
    smem = pl.BlockSpec(memory_space=pltpu.SMEM)
    vmem = pl.BlockSpec(memory_space=pltpu.VMEM)
    return pl.pallas_call(
        exchange_kernel,
        out_shape=jax.ShapeDtypeStruct((slots, local, width), jnp.float32),
        in_specs=[smem, smem, smem, vmem, vmem, vmem],
        out_specs=vmem,
        compiler_params=pltpu.CompilerParams(vmem_limit_bytes=16 << 20),
        name="exchange_terms",
    )(flag_list, pair_counts, place, full, w, wcol)


def shards(ny, pb_total, rows, orbitals, interaction, pair_list, flag_list, pair_counts):
    local, width = orbitals.shape[1:]
    w = interaction[:, 0]
    pieces = orbitals.reshape(ny, local // ny, width)
    pairs = jnp.transpose(pair_list, (0, 2, 1))
    full, wcol = gather(ny, pb_total, rows, pairs, pieces, w)
    full = full.reshape(full.shape[0], rows * local, width)
    place = lax.axis_index("row").astype(jnp.int32).reshape(1)
    return exchange(flag_list, pair_counts, place, full, w, wcol)[None]


def solution(mesh, ny=NY):
    return jax.shard_map(
        functools.partial(shards, ny, mesh.shape["pb"], mesh.shape["row"]),
        mesh=mesh,
        in_specs=(
            P("pb", "row", None),
            P(None, "pb", "row", None),
            P("pb", None, None),
            P("pb", None),
            P("pb"),
        ),
        out_specs=P("pb", None, "row", None),
        check_vma=False,
    )
```

```python
import functools

import jax
import jax.numpy as jnp
from jax import lax
from jax.experimental import pallas as pl
from jax.experimental.pallas import tpu as pltpu
from jax.sharding import PartitionSpec as P

MESH = pl.DeviceIdType.MESH
NY = 4
CORES = 2
LANES = 128
CHUNKS = 2
GROUP = 2


def gather_kernel(
    ny, nz, nx, group,
    pair_hbm, orb_ref, w_hbm,
    full_ref, wcol_ref, w_ref,
    ring, chosen, wsend, idx_send, idx_all, idx_smem, pair_ref,
    idx_ss, idx_rs, piece_ss, piece_rs, z_ss, z_rs, sib_ss, sib_rs, own_ss, own_rs, y_ss, y_rs,
    x_ss, x_rs, hop_ss, hop_rs, core_ss, core_rs, w_ss, w_rs, local_sem,
):
    slots = pair_ref.shape[2]
    wanted = 2 * slots
    pb = lax.axis_index("pb")
    row = lax.axis_index("row")
    y, z = lax.div(pb, nz), lax.rem(pb, nz)
    x, core = lax.div(row, CORES), lax.rem(row, CORES)
    rows = nx * CORES
    stops = nz // group
    stop, seat = lax.div(z, group), lax.rem(z, group)
    kind = lax.rem(row, group)
    base = row - kind
    t_z, t_row = stop * group + kind, base + seat
    same = seat == kind
    moved = jnp.logical_not(same)

    def y_peer(d):
        return lax.rem(y + d, ny)

    def z_peer(d):
        return lax.rem(z + d * group + nz, nz)

    def row_peer(d):
        return lax.rem(row + d, rows)

    def remote(src, dst, ss, rs, to_pb, to_row):
        return pltpu.make_async_remote_copy(
            src_ref=src, dst_ref=dst, send_sem=ss, recv_sem=rs,
            device_id=(to_pb, to_row), device_id_type=MESH,
        )

    pair_load = pltpu.make_async_copy(pair_hbm, pair_ref, local_sem.at[2])
    pair_load.start()
    w_load = pltpu.make_async_copy(w_hbm, w_ref, local_sem.at[3])
    own_piece = pltpu.make_async_copy(orb_ref.at[y], ring.at[seat, stop, y], local_sem.at[4])

    barrier = pltpu.get_barrier_semaphore()
    partners = [(y_peer(d) * nz + t_z, t_row) for d in range(1, ny)]
    ways = (1, -1, 2, -2)
    partners += [(y * nz + z_peer(d), row) for d in ways]
    partners += [(pb, row_peer(d)) for d in range(1, rows)]
    for partner in partners:
        pl.semaphore_signal(barrier, inc=1, device_id=partner, device_id_type=MESH)

    @pl.when(moved)
    def _():
        pl.semaphore_signal(
            barrier, inc=1, device_id=(y * nz + t_z, t_row), device_id_type=MESH
        )
        pl.semaphore_wait(barrier, len(partners) + 1)

    @pl.when(same)
    def _():
        pl.semaphore_wait(barrier, len(partners))

    def to_swap(src, dst, ss, rs, d):
        return remote(src, dst, ss.at[d], rs.at[d], y_peer(d) * nz + t_z, t_row)

    def piece_copy(d):
        return to_swap(orb_ref.at[y_peer(d)], ring.at[seat, stop, y], piece_ss, piece_rs, d)

    def idx_copy(d):
        return to_swap(idx_send, idx_all.at[y], idx_ss, idx_rs, d)

    @pl.when(moved)
    def _():
        piece_copy(0).start()

    for d in range(1, ny):
        piece_copy(d).start()

    @pl.when(same)
    def _():
        own_piece.start()

    w_load.start()
    pair_load.wait()
    lane = lax.broadcasted_iota(jnp.int32, idx_send.shape, 1)
    table = jnp.zeros(idx_send.shape, jnp.int32)
    for j in range(wanted):
        table = jnp.where(lane == j, pair_ref[0, j // slots, j % slots], table)
    idx_send[...] = table

    @pl.when(same)
    def _():
        idx_all[y] = table

    @pl.when(moved)
    def _():
        idx_copy(0).start()

    for d in range(1, ny):
        idx_copy(d).start()

    @pl.when(same)
    def _():
        own_piece.wait()

    @pl.when(moved)
    def _():
        piece_copy(0).wait_recv()

    for d in range(1, ny):
        piece_copy(d).wait_recv()

    half = stops // 2
    width = ny // CHUNKS

    def block_at(way, step):
        return lax.rem(stop - step + stops, stops) if way == 0 else lax.rem(stop + step, stops)

    def z_copy(way, gone, part):
        hop = 2 - lax.rem(gone, 2)
        view = ring.at[kind, block_at(way, gone - hop), pl.ds(part * width, width)]
        return remote(
            view, view, z_ss.at[way, gone - 1, part], z_rs.at[way, gone - 1, part],
            y * nz + z_peer(hop if way == 0 else -hop), row,
        )

    def sibling(d):
        return base + lax.rem(kind + d, group)

    def sib_copy(d, way, step, part):
        view = ring.at[kind, block_at(way, step), pl.ds(part * width, width)]
        return remote(
            view, view, sib_ss.at[d - 1, way, step - 1, part], sib_rs.at[d - 1, way, step - 1, part],
            pb, sibling(d),
        )

    def own_copy(d):
        view = ring.at[kind, stop]
        return remote(view, view, own_ss.at[d - 1], own_rs.at[d - 1], pb, sibling(d))

    others = range(1, group)

    def last(way, part):
        return (part < CHUNKS // 2) == (way == 0)

    pairs = [(way, part) for part in range(CHUNKS) for way in range(2)]
    for hop in (1, 2):
        for way, part in pairs:
            z_copy(way, hop, part).start()
    for d in others:
        own_copy(d).start()

    span, local = w_ref.shape[2] // rows, w_ref.shape[1]
    folds = LANES // (span - LANES)
    fold = local // folds
    w_load.wait()
    for p in range(rows):
        split = p * span + LANES
        wsend[p, :, :local] = w_ref[:, :, p * span : split]
        rest = w_ref[:, :, split : (p + 1) * span].astype(jnp.float32)
        wsend[p, :, local:] = jnp.concatenate(
            [rest[:, f * fold : (f + 1) * fold] for f in range(folds)], axis=2
        ).astype(jnp.bfloat16)

    def w_copy(d):
        to = row_peer(d)
        return remote(wsend.at[to], wcol_ref.at[row], w_ss.at[d - 1], w_rs.at[d - 1], pb, to)

    for d in range(1, rows):
        w_copy(d).start()
    own_columns = pltpu.make_async_copy(wsend.at[row], wcol_ref.at[row], local_sem.at[0])
    own_columns.start()

    def to_siblings(way, gone, part):
        for d in others:
            sib_copy(d, way, gone, part).start()

    def z_step(step, carry):
        gone = 2 * step
        for way, part in pairs:
            z_copy(way, gone, part).wait_recv()
            z_copy(way, gone + 2, part).start()
            z_copy(way, gone + 1, part).start()
            to_siblings(way, gone, part)
        for way, part in pairs:
            z_copy(way, gone - 1, part).wait_recv()
            to_siblings(way, gone - 1, part)
        return carry

    lax.fori_loop(1, half // 2 - 1, z_step, 0)
    for way, part in pairs:
        z_copy(way, half - 2, part).wait_recv()
        if last(way, part):
            z_copy(way, half, part).start()
        z_copy(way, half - 1, part).start()
        to_siblings(way, half - 2, part)
    for gone in (half - 3, half - 1):
        for way, part in pairs:
            z_copy(way, gone, part).wait_recv()
            to_siblings(way, gone, part)

    @pl.when(moved)
    def _():
        idx_copy(0).wait_recv()

    for d in range(1, ny):
        idx_copy(d).wait_recv()
    to_smem = pltpu.make_async_copy(idx_all, idx_smem, local_sem.at[1])
    to_smem.start()
    to_smem.wait()

    for way, part in pairs:
        if last(way, part):
            z_copy(way, half, part).wait_recv()
            to_siblings(way, half, part)

    def sib_wait(step, carry):
        for way, part in pairs:
            for d in others:
                sib_copy(d, way, step, part).wait_recv()
        return carry

    if group > 1:
        for d in others:
            own_copy(d).wait_recv()
        lax.fori_loop(1, half, sib_wait, 0)
        for way, part in pairs:
            if last(way, part):
                for d in others:
                    sib_copy(d, way, half, part).wait_recv()

    def y_copy(d, j):
        return remote(
            chosen.at[d, j], full_ref.at[j, t_row, y], y_ss.at[d, j], y_rs.at[d, j],
            y_peer(d) * nz + t_z, t_row,
        )

    def listed(at, j):
        k = idx_smem[at, 0, j]
        k_z = lax.rem(k, nz)
        return ring[lax.rem(k_z, group), lax.div(k_z, group), lax.div(k, nz)]

    for j in range(wanted):
        for d in range(ny):
            chosen[d, j] = listed(y_peer(d), j)
        for d in range(1, ny):
            y_copy(d, j).start()

        @pl.when(moved)
        def _(j=j):
            y_copy(0, j).start()

        @pl.when(same)
        def _(j=j):
            full_ref[j, row, y] = chosen[0, j]

    other = 1 - core

    def at_x(d):
        return lax.rem(x + d + nx, nx) * CORES + core

    def x_copy(way, j):
        view = full_ref.at[j, row]
        return remote(
            view, view, x_ss.at[way, j], x_rs.at[way, j], pb, at_x(1 if way == 0 else -1)
        )

    def hop_copy(j):
        ahead = 1 if j % 2 == 0 else -1
        view = full_ref.at[j, at_x(-ahead)]
        return remote(view, view, hop_ss.at[j], hop_rs.at[j], pb, at_x(ahead))

    def core_copy(d, j):
        view = full_ref.at[j, at_x(d)]
        return remote(
            view, view, core_ss.at[d, j], core_rs.at[d, j], pb, x * CORES + other
        )

    for j in range(wanted):
        for d in range(1, ny):
            y_copy(d, j).wait_recv()

        @pl.when(moved)
        def _(j=j):
            y_copy(0, j).wait_recv()

        if nx == 4:
            for way in range(2):
                x_copy(way, j).start()
        core_copy(0, j).start()
    if nx == 4:
        for j in range(wanted):
            for way in (0, 1) if j % 2 == 0 else (1, 0):
                x_copy(way, j).wait_recv()
                if way == j % 2:
                    hop_copy(j).start()
                core_copy(3 if way == 0 else 1, j).start()
        for j in range(wanted):
            hop_copy(j).wait_recv()
            core_copy(2, j).start()
    for j in range(wanted):
        for d in range(nx):
            core_copy(d, j).wait_recv()

    own_columns.wait()
    for d in range(1, rows):
        w_copy(d).wait()
    @pl.when(moved)
    def _():
        piece_copy(0).wait_send()
        idx_copy(0).wait_send()
        for j in range(wanted):
            y_copy(0, j).wait_send()

    for d in others:
        own_copy(d).wait_send()
    for d in range(1, ny):
        piece_copy(d).wait_send()
        idx_copy(d).wait_send()
        for j in range(wanted):
            y_copy(d, j).wait_send()

    def z_drain(step, carry):
        for way, part in pairs:
            z_copy(way, step, part).wait_send()
            for d in others:
                sib_copy(d, way, step, part).wait_send()
        return carry

    lax.fori_loop(1, half, z_drain, 0)
    for way, part in pairs:
        if last(way, part):
            z_copy(way, half, part).wait_send()
            for d in others:
                sib_copy(d, way, half, part).wait_send()
    for j in range(wanted):
        if nx == 4:
            for way in range(2):
                x_copy(way, j).wait_send()
            hop_copy(j).wait_send()
        for d in range(nx):
            core_copy(d, j).wait_send()


def gather(ny, pb_total, rows, pair_list, orbitals, w):
    nz, nx = pb_total // ny, rows // CORES
    slots = pair_list.shape[2]
    stops = nz // GROUP
    siblings = max(GROUP - 1, 1)
    piece, width = orbitals.shape[1:]
    span = w.shape[2] // rows
    packed = w.shape[1] * span // LANES
    dma = pltpu.SemaphoreType.DMA
    half = stops // 2
    vmem = pl.BlockSpec(memory_space=pltpu.VMEM)
    return pl.pallas_call(
        functools.partial(gather_kernel, ny, nz, nx, GROUP),
        out_shape=(
            jax.ShapeDtypeStruct((2 * slots, rows, ny, piece, width), jnp.bfloat16),
            jax.ShapeDtypeStruct((rows, 2, packed, LANES), jnp.bfloat16),
            jax.ShapeDtypeStruct(w.shape, w.dtype),
        ),
        in_specs=[pl.BlockSpec(memory_space=pltpu.HBM)] * 3,
        out_specs=(vmem, vmem, vmem),
        scratch_shapes=[
            pltpu.VMEM((GROUP, stops, ny, piece, width), jnp.bfloat16),
            pltpu.VMEM((ny, 2 * slots, piece, width), jnp.bfloat16),
            pltpu.VMEM((rows, 2, packed, LANES), jnp.bfloat16),
            pltpu.VMEM((8, 128), jnp.int32),
            pltpu.VMEM((ny, 8, 128), jnp.int32),
            pltpu.SMEM((ny, 8, 128), jnp.int32),
            pltpu.SMEM(pair_list.shape, jnp.int32),
            dma((ny,)), dma((ny,)),
            dma((ny,)), dma((ny,)),
            dma((2, half, CHUNKS)), dma((2, half, CHUNKS)),
            dma((siblings, 2, half, CHUNKS)), dma((siblings, 2, half, CHUNKS)),
            dma((siblings,)), dma((siblings,)),
            dma((ny, 2 * slots)), dma((ny, 2 * slots)),
            dma((2, 2 * slots)), dma((2, 2 * slots)),
            dma((2 * slots,)), dma((2 * slots,)),
            dma((nx, 2 * slots)), dma((nx, 2 * slots)),
            dma((rows - 1,)), dma((rows - 1,)),
            dma((5,)),
        ],
        compiler_params=pltpu.CompilerParams(collective_id=0, has_side_effects=True, vmem_limit_bytes=16 << 20),
        name="gather_orbitals",
    )(*(pltpu.with_memory_space_constraint(a, pltpu.HBM) for a in (pair_list, orbitals, w)))


def dot_t(a, b):
    return lax.dot_general(a, b, (((1,), (1,)), ((), ())), preferred_element_type=jnp.float32)


def rotate(block):
    half = block.shape[1] // 2
    return jnp.concatenate([block[:, half:], -block[:, :half]], axis=1)


def columns_of(wcol_ref, p, part, local):
    first = wcol_ref[p, part, :local].astype(jnp.float32)
    rest = wcol_ref[p, part, local:].astype(jnp.float32)
    wide = local - LANES
    rest = jnp.concatenate(
        [rest[:, f * wide : (f + 1) * wide] for f in range(LANES // wide)], axis=0
    )
    return jnp.concatenate([first, rest], axis=1)


def exchange_kernel(flag_ref, count_ref, place_ref, full_ref, w_ref, wcol_ref, out_ref):
    slots, local, width = out_ref.shape
    rows = full_ref.shape[1]
    half = width // 2
    total = w_ref.shape[2]
    tile = 256
    me = place_ref[0]

    for s in range(slots):
        live = s < count_ref[0]
        adjoint = flag_ref[0, s] == 1

        @pl.when(jnp.logical_and(live, jnp.logical_not(adjoint)))
        def _(s=s):
            mine = full_ref[slots + s, pl.ds(pl.multiple_of(me * local, local), local), :]
            turned = rotate(mine)
            prod_re = jnp.zeros((local, width), jnp.float32)
            prod_im = jnp.zeros((local, width), jnp.float32)
            for c in range(total // tile):
                cols = pl.ds(c * tile, tile)
                source = full_ref[slots + s, cols, :]
                target = full_ref[s, cols, :]
                d_re = dot_t(mine, source)
                d_im = dot_t(turned, source)
                w_re = w_ref[0, :, cols].astype(jnp.float32)
                w_im = w_ref[1, :, cols].astype(jnp.float32)
                k_re = (w_re * d_re - w_im * d_im).astype(jnp.bfloat16)
                k_im = (w_re * d_im + w_im * d_re).astype(jnp.bfloat16)
                prod_re += jnp.dot(k_re, target, preferred_element_type=jnp.float32)
                prod_im += jnp.dot(k_im, target, preferred_element_type=jnp.float32)
            out_ref[s, :, :half] = prod_re[:, :half] - prod_im[:, half:]
            out_ref[s, :, half:] = prod_re[:, half:] + prod_im[:, :half]

        @pl.when(jnp.logical_and(live, adjoint))
        def _(s=s):
            mine = full_ref[slots + s, pl.ds(pl.multiple_of(me * local, local), local), :]
            prod_re = jnp.zeros((width, local), jnp.float32)
            prod_im = jnp.zeros((width, local), jnp.float32)
            for p in range(wcol_ref.shape[0]):
                cols = pl.ds(p * local, local)
                source = full_ref[slots + s, cols, :]
                target = full_ref[s, cols, :]
                d_re = dot_t(source, mine)
                d_im = dot_t(rotate(source), mine)
                w_re = columns_of(wcol_ref, p, 0, local)
                w_im = columns_of(wcol_ref, p, 1, local)
                k_re = (w_re * d_re - w_im * d_im).astype(jnp.bfloat16)
                k_im = (w_re * d_im + w_im * d_re).astype(jnp.bfloat16)
                flip = target.T
                prod_re += jnp.dot(flip, k_re, preferred_element_type=jnp.float32)
                prod_im += jnp.dot(flip, k_im, preferred_element_type=jnp.float32)
            top = prod_re[:half] + prod_im[half:]
            bottom = prod_re[half:] - prod_im[:half]
            out_ref[s] = jnp.concatenate([top, bottom], axis=0).T

        @pl.when(jnp.logical_not(live))
        def _(s=s):
            out_ref[s] = jnp.zeros((local, width), jnp.float32)


def exchange(flag_list, pair_counts, place, full, w, wcol):
    slots = full.shape[0] // 2
    local, width = w.shape[1], full.shape[2]
    smem = pl.BlockSpec(memory_space=pltpu.SMEM)
    vmem = pl.BlockSpec(memory_space=pltpu.VMEM)
    return pl.pallas_call(
        exchange_kernel,
        out_shape=jax.ShapeDtypeStruct((slots, local, width), jnp.float32),
        in_specs=[smem, smem, smem, vmem, vmem, vmem],
        out_specs=vmem,
        compiler_params=pltpu.CompilerParams(vmem_limit_bytes=16 << 20),
        name="exchange_terms",
    )(flag_list, pair_counts, place, full, w, wcol)


def shards(ny, pb_total, rows, orbitals, interaction, pair_list, flag_list, pair_counts):
    local, width = orbitals.shape[1:]
    w = interaction[:, 0]
    pieces = orbitals.reshape(ny, local // ny, width)
    pairs = jnp.transpose(pair_list, (0, 2, 1))
    full, wcol, w = gather(ny, pb_total, rows, pairs, pieces, w)
    full = full.reshape(full.shape[0], rows * local, width)
    place = lax.axis_index("row").astype(jnp.int32).reshape(1)
    return exchange(flag_list, pair_counts, place, full, w, wcol)[None]


def solution(mesh, ny=NY):
    return jax.shard_map(
        functools.partial(shards, ny, mesh.shape["pb"], mesh.shape["row"]),
        mesh=mesh,
        in_specs=(
            P("pb", "row", None),
            P(None, "pb", "row", None),
            P("pb", None, None),
            P("pb", None),
            P("pb"),
        ),
        out_specs=P("pb", None, "row", None),
        check_vma=False,
    )
```

```python
import functools

import jax
import jax.numpy as jnp
from jax import lax
from jax.experimental import pallas as pl
from jax.experimental.pallas import tpu as pltpu
from jax.sharding import PartitionSpec as P

MESH = pl.DeviceIdType.MESH
NY = 4
CORES = 2
LANES = 128
CHUNKS = 2
GROUP = 2


def gather_kernel(
    ny, nz, nx, group,
    pair_hbm, orb_ref, w_hbm,
    full_ref, wcol_ref, w_ref,
    ring, chosen, wsend, idx_send, idx_all, idx_smem, pair_ref,
    idx_ss, idx_rs, piece_ss, piece_rs, z_ss, z_rs, sib_ss, sib_rs, own_ss, own_rs, y_ss, y_rs,
    x_ss, x_rs, hop_ss, hop_rs, core_ss, core_rs, w_ss, w_rs, local_sem,
):
    slots = pair_ref.shape[2]
    wanted = 2 * slots
    pb = lax.axis_index("pb")
    row = lax.axis_index("row")
    y, z = lax.div(pb, nz), lax.rem(pb, nz)
    x, core = lax.div(row, CORES), lax.rem(row, CORES)
    rows = nx * CORES
    stops = nz // group
    stop, seat = lax.div(z, group), lax.rem(z, group)
    kind = lax.rem(row, group)
    base = row - kind
    t_z, t_row = stop * group + kind, base + seat
    same = seat == kind
    moved = jnp.logical_not(same)

    def y_peer(d):
        return lax.rem(y + d, ny)

    def z_peer(d):
        return lax.rem(z + d * group + nz, nz)

    def row_peer(d):
        return lax.rem(row + d, rows)

    def remote(src, dst, ss, rs, to_pb, to_row):
        return pltpu.make_async_remote_copy(
            src_ref=src, dst_ref=dst, send_sem=ss, recv_sem=rs,
            device_id=(to_pb, to_row), device_id_type=MESH,
        )

    pair_load = pltpu.make_async_copy(pair_hbm, pair_ref, local_sem.at[2])
    pair_load.start()
    w_load = pltpu.make_async_copy(w_hbm, w_ref, local_sem.at[3])
    own_piece = pltpu.make_async_copy(orb_ref.at[y], ring.at[seat, stop, y], local_sem.at[4])

    barrier = pltpu.get_barrier_semaphore()
    partners = [(y_peer(d) * nz + t_z, t_row) for d in range(1, ny)]
    ways = (1, -1, 2, -2)
    partners += [(y * nz + z_peer(d), row) for d in ways]
    partners += [(pb, row_peer(d)) for d in range(1, rows)]
    for partner in partners:
        pl.semaphore_signal(barrier, inc=1, device_id=partner, device_id_type=MESH)

    @pl.when(moved)
    def _():
        pl.semaphore_signal(
            barrier, inc=1, device_id=(y * nz + t_z, t_row), device_id_type=MESH
        )
        pl.semaphore_wait(barrier, len(partners) + 1)

    @pl.when(same)
    def _():
        pl.semaphore_wait(barrier, len(partners))

    def to_swap(src, dst, ss, rs, d):
        return remote(src, dst, ss.at[d], rs.at[d], y_peer(d) * nz + t_z, t_row)

    def piece_copy(d):
        return to_swap(orb_ref.at[y_peer(d)], ring.at[seat, stop, y], piece_ss, piece_rs, d)

    def idx_copy(d):
        return to_swap(idx_send, idx_all.at[y], idx_ss, idx_rs, d)

    @pl.when(moved)
    def _():
        piece_copy(0).start()

    for d in range(1, ny):
        piece_copy(d).start()

    @pl.when(same)
    def _():
        own_piece.start()

    w_load.start()
    pair_load.wait()
    lane = lax.broadcasted_iota(jnp.int32, idx_send.shape, 1)
    table = jnp.zeros(idx_send.shape, jnp.int32)
    for j in range(wanted):
        table = jnp.where(lane == j, pair_ref[0, j // slots, j % slots], table)
    idx_send[...] = table

    @pl.when(same)
    def _():
        idx_all[y] = table

    @pl.when(moved)
    def _():
        idx_copy(0).start()

    for d in range(1, ny):
        idx_copy(d).start()

    @pl.when(same)
    def _():
        own_piece.wait()

    @pl.when(moved)
    def _():
        piece_copy(0).wait_recv()

    for d in range(1, ny):
        piece_copy(d).wait_recv()

    half = stops // 2
    width = ny // CHUNKS

    def block_at(way, step):
        return lax.rem(stop - step + stops, stops) if way == 0 else lax.rem(stop + step, stops)

    def z_copy(way, gone, part):
        hop = 2 - lax.rem(gone, 2)
        view = ring.at[kind, block_at(way, gone - hop), pl.ds(part * width, width)]
        return remote(
            view, view, z_ss.at[way, gone - 1, part], z_rs.at[way, gone - 1, part],
            y * nz + z_peer(hop if way == 0 else -hop), row,
        )

    def sibling(d):
        return base + lax.rem(kind + d, group)

    def sib_copy(d, way, step, part):
        view = ring.at[kind, block_at(way, step), pl.ds(part * width, width)]
        return remote(
            view, view, sib_ss.at[d - 1, way, step - 1, part], sib_rs.at[d - 1, way, step - 1, part],
            pb, sibling(d),
        )

    def own_copy(d):
        view = ring.at[kind, stop]
        return remote(view, view, own_ss.at[d - 1], own_rs.at[d - 1], pb, sibling(d))

    others = range(1, group)

    def last(way, part):
        return (part < CHUNKS // 2) == (way == 0)

    pairs = [(way, part) for part in range(CHUNKS) for way in range(2)]
    for hop in (2, 1):
        for way, part in pairs:
            z_copy(way, hop, part).start()
    for d in others:
        own_copy(d).start()

    span, local = w_ref.shape[2] // rows, w_ref.shape[1]
    folds = LANES // (span - LANES)
    fold = local // folds
    w_load.wait()
    for p in range(rows):
        split = p * span + LANES
        wsend[p, :, :local] = w_ref[:, :, p * span : split]
        rest = w_ref[:, :, split : (p + 1) * span].astype(jnp.float32)
        wsend[p, :, local:] = jnp.concatenate(
            [rest[:, f * fold : (f + 1) * fold] for f in range(folds)], axis=2
        ).astype(jnp.bfloat16)

    def w_copy(d):
        to = row_peer(d)
        return remote(wsend.at[to], wcol_ref.at[row], w_ss.at[d - 1], w_rs.at[d - 1], pb, to)

    for d in range(1, rows):
        w_copy(d).start()
    own_columns = pltpu.make_async_copy(wsend.at[row], wcol_ref.at[row], local_sem.at[0])
    own_columns.start()

    def to_siblings(way, gone, part):
        for d in others:
            sib_copy(d, way, gone, part).start()

    def z_step(step, carry):
        gone = 2 * step
        for way, part in pairs:
            z_copy(way, gone, part).wait_recv()
            z_copy(way, gone + 2, part).start()
        for way, part in pairs:
            z_copy(way, gone + 1, part).start()
            to_siblings(way, gone, part)
        for way, part in pairs:
            z_copy(way, gone - 1, part).wait_recv()
            to_siblings(way, gone - 1, part)
        return carry

    lax.fori_loop(1, half // 2 - 1, z_step, 0)
    for way, part in pairs:
        z_copy(way, half - 2, part).wait_recv()
        if last(way, part):
            z_copy(way, half, part).start()
        z_copy(way, half - 1, part).start()
        to_siblings(way, half - 2, part)
    for gone in (half - 3, half - 1):
        for way, part in pairs:
            z_copy(way, gone, part).wait_recv()
            to_siblings(way, gone, part)

    @pl.when(moved)
    def _():
        idx_copy(0).wait_recv()

    for d in range(1, ny):
        idx_copy(d).wait_recv()
    to_smem = pltpu.make_async_copy(idx_all, idx_smem, local_sem.at[1])
    to_smem.start()
    to_smem.wait()

    for way, part in pairs:
        if last(way, part):
            z_copy(way, half, part).wait_recv()
            to_siblings(way, half, part)

    def sib_wait(step, carry):
        for way, part in pairs:
            for d in others:
                sib_copy(d, way, step, part).wait_recv()
        return carry

    if group > 1:
        for d in others:
            own_copy(d).wait_recv()
        lax.fori_loop(1, half, sib_wait, 0)
        for way, part in pairs:
            if last(way, part):
                for d in others:
                    sib_copy(d, way, half, part).wait_recv()

    def y_copy(d, j):
        return remote(
            chosen.at[d, j], full_ref.at[j, t_row, y], y_ss.at[d, j], y_rs.at[d, j],
            y_peer(d) * nz + t_z, t_row,
        )

    def listed(at, j):
        k = idx_smem[at, 0, j]
        k_z = lax.rem(k, nz)
        return ring[lax.rem(k_z, group), lax.div(k_z, group), lax.div(k, nz)]

    for j in range(wanted):
        for d in range(ny):
            chosen[d, j] = listed(y_peer(d), j)
        for d in sorted(range(1, ny), key=lambda d: -min(d, ny - d)):
            y_copy(d, j).start()

        @pl.when(moved)
        def _(j=j):
            y_copy(0, j).start()

        @pl.when(same)
        def _(j=j):
            full_ref[j, row, y] = chosen[0, j]

    other = 1 - core

    def at_x(d):
        return lax.rem(x + d + nx, nx) * CORES + core

    def x_copy(way, j):
        view = full_ref.at[j, row]
        return remote(
            view, view, x_ss.at[way, j], x_rs.at[way, j], pb, at_x(1 if way == 0 else -1)
        )

    def hop_copy(j):
        ahead = 1 if j % 2 == 0 else -1
        view = full_ref.at[j, at_x(-ahead)]
        return remote(view, view, hop_ss.at[j], hop_rs.at[j], pb, at_x(ahead))

    def core_copy(d, j):
        view = full_ref.at[j, at_x(d)]
        return remote(
            view, view, core_ss.at[d, j], core_rs.at[d, j], pb, x * CORES + other
        )

    for j in range(wanted):
        for d in range(1, ny):
            y_copy(d, j).wait_recv()

        @pl.when(moved)
        def _(j=j):
            y_copy(0, j).wait_recv()

        if nx == 4:
            for way in range(2):
                x_copy(way, j).start()
        core_copy(0, j).start()
    if nx == 4:
        for j in range(wanted):
            for way in (0, 1) if j % 2 == 0 else (1, 0):
                x_copy(way, j).wait_recv()
                if way == j % 2:
                    hop_copy(j).start()
                core_copy(3 if way == 0 else 1, j).start()
        for j in range(wanted):
            hop_copy(j).wait_recv()
            core_copy(2, j).start()
    for j in range(wanted):
        for d in range(nx):
            core_copy(d, j).wait_recv()

    own_columns.wait()
    for d in range(1, rows):
        w_copy(d).wait()
    @pl.when(moved)
    def _():
        piece_copy(0).wait_send()
        idx_copy(0).wait_send()
        for j in range(wanted):
            y_copy(0, j).wait_send()

    for d in others:
        own_copy(d).wait_send()
    for d in range(1, ny):
        piece_copy(d).wait_send()
        idx_copy(d).wait_send()
        for j in range(wanted):
            y_copy(d, j).wait_send()

    def z_drain(step, carry):
        for way, part in pairs:
            z_copy(way, step, part).wait_send()
            for d in others:
                sib_copy(d, way, step, part).wait_send()
        return carry

    lax.fori_loop(1, half, z_drain, 0)
    for way, part in pairs:
        if last(way, part):
            z_copy(way, half, part).wait_send()
            for d in others:
                sib_copy(d, way, half, part).wait_send()
    for j in range(wanted):
        if nx == 4:
            for way in range(2):
                x_copy(way, j).wait_send()
            hop_copy(j).wait_send()
        for d in range(nx):
            core_copy(d, j).wait_send()


def gather(ny, pb_total, rows, pair_list, orbitals, w):
    nz, nx = pb_total // ny, rows // CORES
    slots = pair_list.shape[2]
    stops = nz // GROUP
    siblings = max(GROUP - 1, 1)
    piece, width = orbitals.shape[1:]
    span = w.shape[2] // rows
    packed = w.shape[1] * span // LANES
    dma = pltpu.SemaphoreType.DMA
    half = stops // 2
    vmem = pl.BlockSpec(memory_space=pltpu.VMEM)
    return pl.pallas_call(
        functools.partial(gather_kernel, ny, nz, nx, GROUP),
        out_shape=(
            jax.ShapeDtypeStruct((2 * slots, rows, ny, piece, width), jnp.bfloat16),
            jax.ShapeDtypeStruct((rows, 2, packed, LANES), jnp.bfloat16),
            jax.ShapeDtypeStruct(w.shape, w.dtype),
        ),
        in_specs=[pl.BlockSpec(memory_space=pltpu.HBM)] * 3,
        out_specs=(vmem, vmem, vmem),
        scratch_shapes=[
            pltpu.VMEM((GROUP, stops, ny, piece, width), jnp.bfloat16),
            pltpu.VMEM((ny, 2 * slots, piece, width), jnp.bfloat16),
            pltpu.VMEM((rows, 2, packed, LANES), jnp.bfloat16),
            pltpu.VMEM((8, 128), jnp.int32),
            pltpu.VMEM((ny, 8, 128), jnp.int32),
            pltpu.SMEM((ny, 8, 128), jnp.int32),
            pltpu.SMEM(pair_list.shape, jnp.int32),
            dma((ny,)), dma((ny,)),
            dma((ny,)), dma((ny,)),
            dma((2, half, CHUNKS)), dma((2, half, CHUNKS)),
            dma((siblings, 2, half, CHUNKS)), dma((siblings, 2, half, CHUNKS)),
            dma((siblings,)), dma((siblings,)),
            dma((ny, 2 * slots)), dma((ny, 2 * slots)),
            dma((2, 2 * slots)), dma((2, 2 * slots)),
            dma((2 * slots,)), dma((2 * slots,)),
            dma((nx, 2 * slots)), dma((nx, 2 * slots)),
            dma((rows - 1,)), dma((rows - 1,)),
            dma((5,)),
        ],
        compiler_params=pltpu.CompilerParams(collective_id=0, has_side_effects=True, vmem_limit_bytes=16 << 20),
        name="gather_orbitals",
    )(*(pltpu.with_memory_space_constraint(a, pltpu.HBM) for a in (pair_list, orbitals, w)))


def dot_t(a, b):
    return lax.dot_general(a, b, (((1,), (1,)), ((), ())), preferred_element_type=jnp.float32)


def rotate(block):
    half = block.shape[1] // 2
    return jnp.concatenate([block[:, half:], -block[:, :half]], axis=1)


def columns_of(wcol_ref, p, part, local):
    first = wcol_ref[p, part, :local].astype(jnp.float32)
    rest = wcol_ref[p, part, local:].astype(jnp.float32)
    wide = local - LANES
    rest = jnp.concatenate(
        [rest[:, f * wide : (f + 1) * wide] for f in range(LANES // wide)], axis=0
    )
    return jnp.concatenate([first, rest], axis=1)


def exchange_kernel(flag_ref, count_ref, place_ref, full_ref, w_ref, wcol_ref, out_ref):
    slots, local, width = out_ref.shape
    rows = full_ref.shape[1]
    half = width // 2
    total = w_ref.shape[2]
    tile = 256
    me = place_ref[0]

    for s in range(slots):
        live = s < count_ref[0]
        adjoint = flag_ref[0, s] == 1

        @pl.when(jnp.logical_and(live, jnp.logical_not(adjoint)))
        def _(s=s):
            mine = full_ref[slots + s, pl.ds(pl.multiple_of(me * local, local), local), :]
            both = jnp.concatenate([mine, rotate(mine)], axis=0)
            prod = jnp.zeros((2 * local, width), jnp.float32)
            for c in range(total // tile):
                cols = pl.ds(c * tile, tile)
                source = full_ref[slots + s, cols, :]
                target = full_ref[s, cols, :]
                dens = dot_t(both, source)
                d_re, d_im = dens[:local], dens[local:]
                w_re = w_ref[0, :, cols].astype(jnp.float32)
                w_im = w_ref[1, :, cols].astype(jnp.float32)
                k_re = (w_re * d_re - w_im * d_im).astype(jnp.bfloat16)
                k_im = (w_re * d_im + w_im * d_re).astype(jnp.bfloat16)
                kern = jnp.concatenate([k_re, k_im], axis=0)
                prod += jnp.dot(kern, target, preferred_element_type=jnp.float32)
            prod_re, prod_im = prod[:local], prod[local:]
            out_ref[s, :, :half] = prod_re[:, :half] - prod_im[:, half:]
            out_ref[s, :, half:] = prod_re[:, half:] + prod_im[:, :half]

        @pl.when(jnp.logical_and(live, adjoint))
        def _(s=s):
            mine = full_ref[slots + s, pl.ds(pl.multiple_of(me * local, local), local), :]
            prod_re = jnp.zeros((width, local), jnp.float32)
            prod_im = jnp.zeros((width, local), jnp.float32)
            for p in range(wcol_ref.shape[0]):
                cols = pl.ds(p * local, local)
                source = full_ref[slots + s, cols, :]
                target = full_ref[s, cols, :]
                d_re = dot_t(source, mine)
                d_im = dot_t(rotate(source), mine)
                w_re = columns_of(wcol_ref, p, 0, local)
                w_im = columns_of(wcol_ref, p, 1, local)
                k_re = (w_re * d_re - w_im * d_im).astype(jnp.bfloat16)
                k_im = (w_re * d_im + w_im * d_re).astype(jnp.bfloat16)
                flip = target.T
                prod_re += jnp.dot(flip, k_re, preferred_element_type=jnp.float32)
                prod_im += jnp.dot(flip, k_im, preferred_element_type=jnp.float32)
            top = prod_re[:half] + prod_im[half:]
            bottom = prod_re[half:] - prod_im[:half]
            out_ref[s] = jnp.concatenate([top, bottom], axis=0).T

        @pl.when(jnp.logical_not(live))
        def _(s=s):
            out_ref[s] = jnp.zeros((local, width), jnp.float32)


def exchange(flag_list, pair_counts, place, full, w, wcol):
    slots = full.shape[0] // 2
    local, width = w.shape[1], full.shape[2]
    smem = pl.BlockSpec(memory_space=pltpu.SMEM)
    vmem = pl.BlockSpec(memory_space=pltpu.VMEM)
    return pl.pallas_call(
        exchange_kernel,
        out_shape=jax.ShapeDtypeStruct((slots, local, width), jnp.float32),
        in_specs=[smem, smem, smem, vmem, vmem, vmem],
        out_specs=vmem,
        compiler_params=pltpu.CompilerParams(vmem_limit_bytes=16 << 20),
        name="exchange_terms",
    )(
        pltpu.with_memory_space_constraint(flag_list, pltpu.HBM),
        pair_counts, place, full, w, wcol,
    )


def shards(ny, pb_total, rows, orbitals, interaction, pair_list, flag_list, pair_counts):
    local, width = orbitals.shape[1:]
    w = interaction[:, 0]
    pieces = orbitals.reshape(ny, local // ny, width)
    pairs = jnp.transpose(pair_list, (0, 2, 1))
    full, wcol, w = gather(ny, pb_total, rows, pairs, pieces, w)
    full = full.reshape(full.shape[0], rows * local, width)
    place = lax.axis_index("row").astype(jnp.int32).reshape(1)
    return exchange(flag_list, pair_counts, place, full, w, wcol)[None]


def solution(mesh, ny=NY):
    return jax.shard_map(
        functools.partial(shards, ny, mesh.shape["pb"], mesh.shape["row"]),
        mesh=mesh,
        in_specs=(
            P("pb", "row", None),
            P(None, "pb", "row", None),
            P("pb", None, None),
            P("pb", None),
            P("pb"),
        ),
        out_specs=P("pb", None, "row", None),
        check_vma=False,
    )
```

```python
import functools

import jax
import jax.numpy as jnp
from jax import lax
from jax.experimental import pallas as pl
from jax.experimental.pallas import tpu as pltpu
from jax.sharding import PartitionSpec as P

MESH = pl.DeviceIdType.MESH
NY = 4
CORES = 2
LANES = 128
CHUNKS = 2
GROUP = 2


def gather_kernel(
    ny, nz, nx, group,
    pair_hbm, orb_ref, w_hbm,
    full_ref, wcol_ref, w_ref,
    ring, chosen, wsend, idx_send, idx_all, idx_smem, pair_ref,
    idx_ss, idx_rs, piece_ss, piece_rs, z_ss, z_rs, sib_ss, sib_rs, own_ss, own_rs, y_ss, y_rs,
    x_ss, x_rs, hop_ss, hop_rs, core_ss, core_rs, w_ss, w_rs, local_sem,
):
    slots = pair_ref.shape[2]
    wanted = 2 * slots
    pb = lax.axis_index("pb")
    row = lax.axis_index("row")
    y, z = lax.div(pb, nz), lax.rem(pb, nz)
    x, core = lax.div(row, CORES), lax.rem(row, CORES)
    rows = nx * CORES
    stops = nz // group
    stop, seat = lax.div(z, group), lax.rem(z, group)
    kind = lax.rem(row, group)
    base = row - kind
    t_z, t_row = stop * group + kind, base + seat
    same = seat == kind
    moved = jnp.logical_not(same)

    def y_peer(d):
        return lax.rem(y + d, ny)

    def z_peer(d):
        return lax.rem(z + d * group + nz, nz)

    def row_peer(d):
        return lax.rem(row + d, rows)

    def remote(src, dst, ss, rs, to_pb, to_row):
        return pltpu.make_async_remote_copy(
            src_ref=src, dst_ref=dst, send_sem=ss, recv_sem=rs,
            device_id=(to_pb, to_row), device_id_type=MESH,
        )

    pair_load = pltpu.make_async_copy(pair_hbm, pair_ref, local_sem.at[2])
    pair_load.start()
    w_load = pltpu.make_async_copy(w_hbm, w_ref, local_sem.at[3])
    own_piece = pltpu.make_async_copy(orb_ref.at[y], ring.at[seat, stop, y], local_sem.at[4])

    barrier = pltpu.get_barrier_semaphore()
    partners = [(y_peer(d) * nz + t_z, t_row) for d in range(1, ny)]
    ways = (1, -1, 2, -2)
    partners += [(y * nz + z_peer(d), row) for d in ways]
    partners += [(pb, row_peer(d)) for d in range(1, rows)]
    for partner in partners:
        pl.semaphore_signal(barrier, inc=1, device_id=partner, device_id_type=MESH)

    @pl.when(moved)
    def _():
        pl.semaphore_signal(
            barrier, inc=1, device_id=(y * nz + t_z, t_row), device_id_type=MESH
        )
        pl.semaphore_wait(barrier, len(partners) + 1)

    @pl.when(same)
    def _():
        pl.semaphore_wait(barrier, len(partners))

    def to_swap(src, dst, ss, rs, d):
        return remote(src, dst, ss.at[d], rs.at[d], y_peer(d) * nz + t_z, t_row)

    def piece_copy(d):
        return to_swap(orb_ref.at[y_peer(d)], ring.at[seat, stop, y], piece_ss, piece_rs, d)

    def idx_copy(d):
        return to_swap(idx_send, idx_all.at[y], idx_ss, idx_rs, d)

    @pl.when(moved)
    def _():
        piece_copy(0).start()

    for d in range(1, ny):
        piece_copy(d).start()

    @pl.when(same)
    def _():
        own_piece.start()

    w_load.start()
    pair_load.wait()
    lane = lax.broadcasted_iota(jnp.int32, idx_send.shape, 1)
    table = jnp.zeros(idx_send.shape, jnp.int32)
    for j in range(wanted):
        table = jnp.where(lane == j, pair_ref[0, j // slots, j % slots], table)
    idx_send[...] = table

    @pl.when(same)
    def _():
        idx_all[y] = table

    @pl.when(moved)
    def _():
        idx_copy(0).start()

    for d in range(1, ny):
        idx_copy(d).start()

    @pl.when(same)
    def _():
        own_piece.wait()

    @pl.when(moved)
    def _():
        piece_copy(0).wait_recv()

    for d in range(1, ny):
        piece_copy(d).wait_recv()

    half = stops // 2
    width = ny // CHUNKS

    def block_at(way, step):
        return lax.rem(stop - step + stops, stops) if way == 0 else lax.rem(stop + step, stops)

    def z_copy(way, gone, part):
        hop = 2 - lax.rem(gone, 2)
        view = ring.at[kind, block_at(way, gone - hop), pl.ds(part * width, width)]
        return remote(
            view, view, z_ss.at[way, gone - 1, part], z_rs.at[way, gone - 1, part],
            y * nz + z_peer(hop if way == 0 else -hop), row,
        )

    def sibling(d):
        return base + lax.rem(kind + d, group)

    def sib_copy(d, way, step, part):
        view = ring.at[kind, block_at(way, step), pl.ds(part * width, width)]
        return remote(
            view, view, sib_ss.at[d - 1, way, step - 1, part], sib_rs.at[d - 1, way, step - 1, part],
            pb, sibling(d),
        )

    def own_copy(d):
        view = ring.at[kind, stop]
        return remote(view, view, own_ss.at[d - 1], own_rs.at[d - 1], pb, sibling(d))

    others = range(1, group)

    def last(way, part):
        return (part < CHUNKS // 2) == (way == 0)

    pairs = [(way, part) for part in range(CHUNKS) for way in range(2)]
    for hop in (2, 1):
        for way, part in pairs:
            z_copy(way, hop, part).start()
    for d in others:
        own_copy(d).start()

    span, local = w_ref.shape[2] // rows, w_ref.shape[1]
    folds = LANES // (span - LANES)
    fold = local // folds
    w_load.wait()
    for p in range(rows):
        split = p * span + LANES
        wsend[p, :, :local] = w_ref[:, :, p * span : split]
        rest = w_ref[:, :, split : (p + 1) * span].astype(jnp.float32)
        wsend[p, :, local:] = jnp.concatenate(
            [rest[:, f * fold : (f + 1) * fold] for f in range(folds)], axis=2
        ).astype(jnp.bfloat16)

    def w_copy(d):
        to = row_peer(d)
        return remote(wsend.at[to], wcol_ref.at[row], w_ss.at[d - 1], w_rs.at[d - 1], pb, to)

    for d in range(1, rows):
        w_copy(d).start()
    own_columns = pltpu.make_async_copy(wsend.at[row], wcol_ref.at[row], local_sem.at[0])
    own_columns.start()

    @pl.when(moved)
    def _():
        idx_copy(0).wait_recv()

    for d in range(1, ny):
        idx_copy(d).wait_recv()
    to_smem = pltpu.make_async_copy(idx_all, idx_smem, local_sem.at[1])
    to_smem.start()

    def to_siblings(way, gone, part):
        for d in others:
            sib_copy(d, way, gone, part).start()

    def z_step(step, carry):
        gone = 2 * step
        for way, part in pairs:
            z_copy(way, gone, part).wait_recv()
            z_copy(way, gone + 2, part).start()
        for way, part in pairs:
            z_copy(way, gone + 1, part).start()
            to_siblings(way, gone, part)
        for way, part in pairs:
            z_copy(way, gone - 1, part).wait_recv()
            to_siblings(way, gone - 1, part)
        return carry

    lax.fori_loop(1, half // 2 - 1, z_step, 0)
    for way, part in pairs:
        z_copy(way, half - 2, part).wait_recv()
        if last(way, part):
            z_copy(way, half, part).start()
        z_copy(way, half - 1, part).start()
        to_siblings(way, half - 2, part)
    for gone in (half - 3, half - 1):
        for way, part in pairs:
            z_copy(way, gone, part).wait_recv()
            to_siblings(way, gone, part)

    to_smem.wait()

    for way, part in pairs:
        if last(way, part):
            z_copy(way, half, part).wait_recv()
            to_siblings(way, half, part)

    def sib_wait(step, carry):
        for way, part in pairs:
            for d in others:
                sib_copy(d, way, step, part).wait_recv()
        return carry

    if group > 1:
        for d in others:
            own_copy(d).wait_recv()
        lax.fori_loop(1, half, sib_wait, 0)
        for way, part in pairs:
            if last(way, part):
                for d in others:
                    sib_copy(d, way, half, part).wait_recv()

    def y_copy(d, j):
        return remote(
            chosen.at[d, j], full_ref.at[j, t_row, y], y_ss.at[d, j], y_rs.at[d, j],
            y_peer(d) * nz + t_z, t_row,
        )

    def listed(at, j):
        k = idx_smem[at, 0, j]
        k_z = lax.rem(k, nz)
        return ring[lax.rem(k_z, group), lax.div(k_z, group), lax.div(k, nz)]

    for j in range(wanted):
        for d in range(ny):
            chosen[d, j] = listed(y_peer(d), j)
        for d in sorted(range(1, ny), key=lambda d: -min(d, ny - d)):
            y_copy(d, j).start()

        @pl.when(moved)
        def _(j=j):
            y_copy(0, j).start()

        @pl.when(same)
        def _(j=j):
            full_ref[j, row, y] = chosen[0, j]

    other = 1 - core

    def at_x(d):
        return lax.rem(x + d + nx, nx) * CORES + core

    def x_copy(way, j):
        view = full_ref.at[j, row]
        return remote(
            view, view, x_ss.at[way, j], x_rs.at[way, j], pb, at_x(1 if way == 0 else -1)
        )

    def hop_copy(j):
        ahead = 1 if j % 2 == 0 else -1
        view = full_ref.at[j, at_x(-ahead)]
        return remote(view, view, hop_ss.at[j], hop_rs.at[j], pb, at_x(ahead))

    def core_copy(d, j):
        view = full_ref.at[j, at_x(d)]
        return remote(
            view, view, core_ss.at[d, j], core_rs.at[d, j], pb, x * CORES + other
        )

    for j in range(wanted):
        for d in range(1, ny):
            y_copy(d, j).wait_recv()

        @pl.when(moved)
        def _(j=j):
            y_copy(0, j).wait_recv()

        if nx == 4:
            for way in range(2):
                x_copy(way, j).start()
        core_copy(0, j).start()
    if nx == 4:
        for j in range(wanted):
            for way in (0, 1) if j % 2 == 0 else (1, 0):
                x_copy(way, j).wait_recv()
                if way == j % 2:
                    hop_copy(j).start()
                core_copy(3 if way == 0 else 1, j).start()
        for j in range(wanted):
            hop_copy(j).wait_recv()
            core_copy(2, j).start()
    for j in range(wanted):
        for d in range(nx):
            core_copy(d, j).wait_recv()

    own_columns.wait()
    for d in range(1, rows):
        w_copy(d).wait()
    @pl.when(moved)
    def _():
        piece_copy(0).wait_send()
        idx_copy(0).wait_send()
        for j in range(wanted):
            y_copy(0, j).wait_send()

    for d in others:
        own_copy(d).wait_send()
    for d in range(1, ny):
        piece_copy(d).wait_send()
        idx_copy(d).wait_send()
        for j in range(wanted):
            y_copy(d, j).wait_send()

    def z_drain(step, carry):
        for way, part in pairs:
            z_copy(way, step, part).wait_send()
            for d in others:
                sib_copy(d, way, step, part).wait_send()
        return carry

    lax.fori_loop(1, half, z_drain, 0)
    for way, part in pairs:
        if last(way, part):
            z_copy(way, half, part).wait_send()
            for d in others:
                sib_copy(d, way, half, part).wait_send()
    for j in range(wanted):
        if nx == 4:
            for way in range(2):
                x_copy(way, j).wait_send()
            hop_copy(j).wait_send()
        for d in range(nx):
            core_copy(d, j).wait_send()


def gather(ny, pb_total, rows, pair_list, orbitals, w):
    nz, nx = pb_total // ny, rows // CORES
    slots = pair_list.shape[2]
    stops = nz // GROUP
    siblings = max(GROUP - 1, 1)
    piece, width = orbitals.shape[1:]
    span = w.shape[2] // rows
    packed = w.shape[1] * span // LANES
    dma = pltpu.SemaphoreType.DMA
    half = stops // 2
    vmem = pl.BlockSpec(memory_space=pltpu.VMEM)
    return pl.pallas_call(
        functools.partial(gather_kernel, ny, nz, nx, GROUP),
        out_shape=(
            jax.ShapeDtypeStruct((2 * slots, rows, ny, piece, width), jnp.bfloat16),
            jax.ShapeDtypeStruct((rows, 2, packed, LANES), jnp.bfloat16),
            jax.ShapeDtypeStruct(w.shape, w.dtype),
        ),
        in_specs=[pl.BlockSpec(memory_space=pltpu.HBM)] * 3,
        out_specs=(vmem, vmem, vmem),
        scratch_shapes=[
            pltpu.VMEM((GROUP, stops, ny, piece, width), jnp.bfloat16),
            pltpu.VMEM((ny, 2 * slots, piece, width), jnp.bfloat16),
            pltpu.VMEM((rows, 2, packed, LANES), jnp.bfloat16),
            pltpu.VMEM((8, 128), jnp.int32),
            pltpu.VMEM((ny, 8, 128), jnp.int32),
            pltpu.SMEM((ny, 8, 128), jnp.int32),
            pltpu.SMEM(pair_list.shape, jnp.int32),
            dma((ny,)), dma((ny,)),
            dma((ny,)), dma((ny,)),
            dma((2, half, CHUNKS)), dma((2, half, CHUNKS)),
            dma((siblings, 2, half, CHUNKS)), dma((siblings, 2, half, CHUNKS)),
            dma((siblings,)), dma((siblings,)),
            dma((ny, 2 * slots)), dma((ny, 2 * slots)),
            dma((2, 2 * slots)), dma((2, 2 * slots)),
            dma((2 * slots,)), dma((2 * slots,)),
            dma((nx, 2 * slots)), dma((nx, 2 * slots)),
            dma((rows - 1,)), dma((rows - 1,)),
            dma((5,)),
        ],
        compiler_params=pltpu.CompilerParams(collective_id=0, has_side_effects=True, vmem_limit_bytes=16 << 20),
        name="gather_orbitals",
    )(*(pltpu.with_memory_space_constraint(a, pltpu.HBM) for a in (pair_list, orbitals, w)))


def dot_t(a, b):
    return lax.dot_general(a, b, (((1,), (1,)), ((), ())), preferred_element_type=jnp.float32)


def rotate(block):
    half = block.shape[1] // 2
    return jnp.concatenate([block[:, half:], -block[:, :half]], axis=1)


def columns_of(wcol_ref, p, part, local):
    first = wcol_ref[p, part, :local].astype(jnp.float32)
    rest = wcol_ref[p, part, local:].astype(jnp.float32)
    wide = local - LANES
    rest = jnp.concatenate(
        [rest[:, f * wide : (f + 1) * wide] for f in range(LANES // wide)], axis=0
    )
    return jnp.concatenate([first, rest], axis=1)


def exchange_kernel(flag_ref, count_ref, place_ref, full_ref, w_ref, wcol_ref, out_ref):
    slots, local, width = out_ref.shape
    rows = full_ref.shape[1]
    half = width // 2
    total = w_ref.shape[2]
    tile = 256
    me = place_ref[0]

    for s in range(slots):
        live = s < count_ref[0]
        adjoint = flag_ref[0, s] == 1

        @pl.when(jnp.logical_and(live, jnp.logical_not(adjoint)))
        def _(s=s):
            mine = full_ref[slots + s, pl.ds(pl.multiple_of(me * local, local), local), :]
            both = jnp.concatenate([mine, rotate(mine)], axis=0)
            prod = jnp.zeros((2 * local, width), jnp.float32)
            for c in range(total // tile):
                cols = pl.ds(c * tile, tile)
                source = full_ref[slots + s, cols, :]
                target = full_ref[s, cols, :]
                dens = dot_t(both, source)
                d_re, d_im = dens[:local], dens[local:]
                w_re = w_ref[0, :, cols].astype(jnp.float32)
                w_im = w_ref[1, :, cols].astype(jnp.float32)
                k_re = (w_re * d_re - w_im * d_im).astype(jnp.bfloat16)
                k_im = (w_re * d_im + w_im * d_re).astype(jnp.bfloat16)
                kern = jnp.concatenate([k_re, k_im], axis=0)
                prod += jnp.dot(kern, target, preferred_element_type=jnp.float32)
            prod_re, prod_im = prod[:local], prod[local:]
            out_ref[s, :, :half] = prod_re[:, :half] - prod_im[:, half:]
            out_ref[s, :, half:] = prod_re[:, half:] + prod_im[:, :half]

        @pl.when(jnp.logical_and(live, adjoint))
        def _(s=s):
            mine = full_ref[slots + s, pl.ds(pl.multiple_of(me * local, local), local), :]
            prod_re = jnp.zeros((width, local), jnp.float32)
            prod_im = jnp.zeros((width, local), jnp.float32)
            for p in range(wcol_ref.shape[0]):
                cols = pl.ds(p * local, local)
                source = full_ref[slots + s, cols, :]
                target = full_ref[s, cols, :]
                both = jnp.concatenate([source, rotate(source)], axis=0)
                dens = dot_t(both, mine)
                d_re, d_im = dens[:local], dens[local:]
                w_re = columns_of(wcol_ref, p, 0, local)
                w_im = columns_of(wcol_ref, p, 1, local)
                k_re = (w_re * d_re - w_im * d_im).astype(jnp.bfloat16)
                k_im = (w_re * d_im + w_im * d_re).astype(jnp.bfloat16)
                flip = target.T
                prod_re += jnp.dot(flip, k_re, preferred_element_type=jnp.float32)
                prod_im += jnp.dot(flip, k_im, preferred_element_type=jnp.float32)
            top = prod_re[:half] + prod_im[half:]
            bottom = prod_re[half:] - prod_im[:half]
            out_ref[s] = jnp.concatenate([top, bottom], axis=0).T

        @pl.when(jnp.logical_not(live))
        def _(s=s):
            out_ref[s] = jnp.zeros((local, width), jnp.float32)


def exchange(flag_list, pair_counts, place, full, w, wcol):
    slots = full.shape[0] // 2
    local, width = w.shape[1], full.shape[2]
    smem = pl.BlockSpec(memory_space=pltpu.SMEM)
    vmem = pl.BlockSpec(memory_space=pltpu.VMEM)
    return pl.pallas_call(
        exchange_kernel,
        out_shape=jax.ShapeDtypeStruct((slots, local, width), jnp.float32),
        in_specs=[smem, smem, smem, vmem, vmem, vmem],
        out_specs=vmem,
        compiler_params=pltpu.CompilerParams(vmem_limit_bytes=16 << 20),
        name="exchange_terms",
    )(
        pltpu.with_memory_space_constraint(flag_list, pltpu.HBM),
        pair_counts, place, full, w, wcol,
    )


def shards(ny, pb_total, rows, orbitals, interaction, pair_list, flag_list, pair_counts):
    local, width = orbitals.shape[1:]
    w = interaction[:, 0]
    pieces = orbitals.reshape(ny, local // ny, width)
    pairs = jnp.transpose(pair_list, (0, 2, 1))
    full, wcol, w = gather(ny, pb_total, rows, pairs, pieces, w)
    full = full.reshape(full.shape[0], rows * local, width)
    place = lax.axis_index("row").astype(jnp.int32).reshape(1)
    return exchange(flag_list, pair_counts, place, full, w, wcol)[None]


def solution(mesh, ny=NY):
    return jax.shard_map(
        functools.partial(shards, ny, mesh.shape["pb"], mesh.shape["row"]),
        mesh=mesh,
        in_specs=(
            P("pb", "row", None),
            P(None, "pb", "row", None),
            P("pb", None, None),
            P("pb", None),
            P("pb"),
        ),
        out_specs=P("pb", None, "row", None),
        check_vma=False,
    )
```
